128 devices in a mesh: blk: 8 (over z, x_lo), tp: 16 (over x_hi, y, core).
Axes of the slice: x: 4 (x_hi: 2, x_lo: 2; x = x_hi * 2 + x_lo), y: 4, z: 4, core: 2. Of those that a mesh axis runs over, the one named last changes fastest.
Arguments:
- input_pool: bfloat16 [4096, 1792], P(None, 'tp'), may hold values from -6 to 6
- teacher_pool: bfloat16 [4096, 1792], P(None, 'tp'), may hold values from -6 to 6
- gate_weight: bfloat16 [1792, 9472], P(None, 'tp'), may hold values from -0.125 to 0.125
- up_weight: bfloat16 [1792, 9472], P(None, 'tp'), may hold values from -0.125 to 0.125
- params: float32 [8, 9472, 1792], P('blk', 'tp'), may hold values from -6 to 6
- batch_ids: int32 [8, 1024], replicated, may hold values from 0 to 4095
- cycle_order: int32 [8], replicated, may hold values from 0 to 7, each once
- edge_weight: float32 [8], replicated, may hold values from 0.1 to 0.45
Outputs:
- updated: float32 [8, 9472, 1792], P('blk', 'tp')
The draws below stay inside these ranges and needn't reach their ends.
Inputs may be any that keep to these rules, and one draw needn't show every extreme that they name: `cycle_order`: the 8 cycle positions name 8 different agents.
All inputs are finite; a program needn't handle non-finite values.
Results may differ from the reference program's by a relative error of at most 0.0061.
Values may be sent and summed in bfloat16 or wider, within the bound.
No kernel may reach another device: no remote copies, remote signals or barrier semaphores. Data moves between devices by JAX's collectives and lax.ppermute only.
A program may use at most 128 MiB of HBM per device.

```python
import math
import jax
import jax.numpy as jnp
from jax import lax

D = 1792
FF = 9472
TOK = 1024
POOL = 4096
AGENTS = 8


def set_ends(entries, key, least, top_value):
    index_at = [jax.random.randint(jax.random.fold_in(key, axis), (), 0, length) for axis, length in enumerate(entries.shape)]
    widest = entries.shape.index(max(entries.shape))
    next_to = index_at[:widest] + [(index_at[widest] + 1) % entries.shape[widest]] + index_at[widest + 1:]
    return entries.at[tuple(index_at)].set(least).at[tuple(next_to)].set(top_value)


def block_scale(stream_key, shape, cuts, smallest, largest):
    def one(axis_at, shards_of):
        draws = jax.random.uniform(jax.random.fold_in(jax.random.fold_in(stream_key, 6), axis_at), (shards_of,), jnp.float32, smallest / len(cuts), largest / len(cuts))
        return jnp.repeat(jnp.exp(draws), shape[axis_at] // shards_of).reshape((-1,) + (1,) * (len(shape) - axis_at - 1))

    loudness = one(*cuts[0])
    for cut in cuts[1:]:
        loudness = loudness * one(*cut)
    return loudness


def scatter_about(stream_key, shape, width, limit, split=(), dtype=jnp.bfloat16):
    result = jax.random.normal(stream_key, shape, jnp.float32) * width
    if len(split) > 0:
        result = block_scale(stream_key, shape, split, -0.22, 0.18) * result
    return jnp.clip(result, min=-limit, max=limit).astype(dtype)


def setup_inputs(seed: int = 0) -> dict:
    splits = jax.random.split(jax.random.key(seed), 9)
    input_pool = scatter_about(splits[0], (POOL, D), 1.0, 6.0, ((1, 16),))
    teacher_pool = scatter_about(splits[1], (POOL, D), 1.0, 6.0, ((1, 16),))
    gate_weight = scatter_about(splits[2], (D, FF), D ** -0.5, 0.125, ((1, 16),))
    up_weight = scatter_about(splits[3], (D, FF), D ** -0.5, 0.125, ((1, 16),))
    params = scatter_about(splits[4], (AGENTS, FF, D), 1.0, 6.0, ((0, 8), (1, 16)), jnp.float32)
    batch_ids = set_ends(jax.random.randint(splits[5], (AGENTS, TOK), 0, POOL), jax.random.fold_in(splits[5], 1), 0, POOL - 1).astype(jnp.int32)
    cycle_order = jax.random.permutation(splits[6], AGENTS).astype(jnp.int32)
    edge_weight = jnp.clip(jnp.exp(jax.random.uniform(splits[7], (AGENTS,), jnp.float32, math.log(0.1), math.log(0.45))), 0.1, 0.45)
    return {"input_pool": input_pool, "teacher_pool": teacher_pool, "gate_weight": gate_weight, "up_weight": up_weight, "params": params, "batch_ids": batch_ids, "cycle_order": cycle_order, "edge_weight": edge_weight}


def reference(input_pool, teacher_pool, gate_weight, up_weight, params, batch_ids, cycle_order, edge_weight):
    scale = float(FF) ** (-0.5)
    step_rate = 2.0
    batches = batch_ids[cycle_order]

    def make_hidden(batch):
        rows = input_pool[batch]
        gate = jnp.dot(rows, gate_weight, preferred_element_type=jnp.float32)
        up = jnp.dot(rows, up_weight, preferred_element_type=jnp.float32)
        return (jax.nn.silu(gate) * up).astype(jnp.bfloat16)
    hidden = lax.map(make_hidden, batches)
    targets = teacher_pool[batches]

    def one_grad(items):
        hid, tgt, weights = items
        out = scale * jnp.dot(hid, weights.astype(jnp.bfloat16), preferred_element_type=jnp.float32)
        resid = (out - tgt.astype(jnp.float32)).astype(jnp.bfloat16)
        return scale * jnp.dot(hid.T, resid, preferred_element_type=jnp.float32)

    def gradient(field):
        return lax.map(one_grad, (hidden, targets, field))
    weight_next = edge_weight[:, None, None]
    weight_prev = jnp.roll(edge_weight, 1)[:, None, None]
    weight_self = 1.0 - weight_next - weight_prev

    def mix(field):
        return weight_self * field + weight_next * jnp.roll(field, -1, 0) + weight_prev * jnp.roll(field, 1, 0)
    grad_first = gradient(params)
    moved = mix(params) - step_rate * grad_first
    grad_second = gradient(moved)
    tracker = mix(grad_first) + grad_second - grad_first
    return mix(moved) - step_rate * tracker
```

```python
import jax
import jax.numpy as jnp
from jax import lax
from jax.experimental import pallas as pl
from jax.experimental.pallas import tpu as pltpu
from jax.sharding import PartitionSpec as P


NX, NY, NC = 2, 4, 2
CHUNKS = 2
BF = jnp.bfloat16
F32 = jnp.float32


def tp_shift(dx, dy, dc):
    pairs = []
    for x in range(NX):
        for y in range(NY):
            for c in range(NC):
                to = ((x + dx) % NX * NY + (y + dy) % NY) * NC + (c + dc) % NC
                pairs.append(((x * NY + y) * NC + c, to))
    return pairs


def send(array, dx, dy, dc):
    return lax.ppermute(array, "tp", tp_shift(dx, dy, dc))


def permute_kernel(index_ref, *refs):
    half = len(refs) // 2
    for source, out in zip(refs[:half], refs[half:]):
        out[...] = source[...]


def permute_rows(arrays, index, count):
    specs_in, specs_out, shapes = [], [], []
    for a in arrays:
        block = (a.shape[0] // count, a.shape[1])
        specs_in.append(pl.BlockSpec(block, lambda i, index: (index[i], 0)))
        specs_out.append(pl.BlockSpec(block, lambda i, index: (i, 0)))
        shapes.append(jax.ShapeDtypeStruct(a.shape, a.dtype))
    size = sum(a.size * a.dtype.itemsize for a in arrays)
    return pl.pallas_call(
        permute_kernel,
        out_shape=shapes,
        grid_spec=pltpu.PrefetchScalarGridSpec(
            num_scalar_prefetch=1, grid=(count,), in_specs=specs_in, out_specs=specs_out
        ),
        cost_estimate=pl.CostEstimate(flops=0, transcendentals=0, bytes_accessed=2 * size),
        name="permute_rows",
    )(index, *arrays)


def gather_blocks(own):
    pair = jnp.concatenate([own, send(own, 1, 0, 0)], axis=0)
    parts = [pair, send(pair, 0, -1, 0), send(pair, 0, -2, 0), send(pair, 0, -3, 0)]
    plane = jnp.concatenate(parts, axis=0)
    return jnp.concatenate([plane, send(plane, 0, 0, 1)], axis=0)


def add(*terms):
    total = terms[0].astype(F32)
    for term in terms[1:]:
        total = total + term.astype(F32)
    return total.astype(BF)


def scatter_sum(partial):
    half = partial.shape[0] // 2
    mine = add(partial[:half], send(partial[half:], 0, 0, 1))
    quarter = half // NY
    got = [send(mine[d * quarter : (d + 1) * quarter], 0, d, 0) for d in (1, 2, 3)]
    mine = add(mine[:quarter], *got)
    last = quarter // NX
    return add(mine[:last], send(mine[last:], 1, 0, 0))


def body(
    input_pool, teacher_pool, gate_weight, up_weight, params, batch_ids, cycle_order, edge_weight
):
    step = 2.0
    groups = lax.axis_size("tp")
    agents = cycle_order.shape[0]
    place = lax.axis_index("blk")
    at = lax.axis_index("tp")
    core, y, xh = at % NC, (at // NC) % NY, at // (NC * NY)
    slots = jnp.arange(agents, dtype=jnp.int32)

    def edge(offset):
        return jnp.sum(jnp.where(slots == (place + offset) % agents, edge_weight, 0.0))

    weight_next, weight_prev = edge(0), edge(agents - 1)
    weight_self = 1.0 - weight_next - weight_prev
    odd = place % 2 == 1
    coef_own = jnp.where(odd, weight_prev, weight_next)
    coef_got = jnp.where(odd, edge(agents - 2), edge(1))
    agent = jnp.sum(jnp.where(slots == place, cycle_order, 0))
    batch = lax.dynamic_slice_in_dim(batch_ids, agent, 1, 0)[0]

    order = jnp.arange(groups, dtype=jnp.int32)
    dc, dy, dx = order // (NY * NX), (order // NX) % NY, order % NX
    c_at, y_at, x_at = (core + dc) % NC, (y + dy) % NY, (xh + dx) % NX
    feature_order = (x_at * NY + y_at) * NC + c_at
    token_order = (c_at * NY + y_at) * NX + x_at

    rows = jnp.take(input_pool, batch, axis=0).T
    inputs = gather_blocks(rows)
    gate_rel, up_rel = permute_rows([gate_weight, up_weight], feature_order, groups)
    batch_rel = jnp.take(batch.reshape(groups, -1), token_order, axis=0).reshape(-1)
    teacher = jnp.take(teacher_pool, batch_rel, axis=0)
    width = teacher.shape[1]
    features = width * groups
    place_in = (
        lax.broadcasted_iota(jnp.int32, (width, features), 0) + at * width
        == lax.broadcasted_iota(jnp.int32, (width, features), 1)
    ).astype(BF)
    teacher_wide = jnp.dot(teacher, place_in, preferred_element_type=F32).astype(BF)

    hidden_dev = gate_weight.shape[1]
    scale = float(hidden_dev * groups) ** (-0.5)
    cut = features // CHUNKS
    cols = [slice(i * cut, (i + 1) * cut) for i in range(CHUNKS)]
    field = [params[0][:, s] for s in cols]
    teach = [teacher_wide[:, s] for s in cols]

    def along_z(a):
        return lax.ppermute(
            a, "blk", [(i, (i + 2) % agents if i % 2 else (i - 2) % agents) for i in range(agents)]
        )

    def along_x(a):
        return lax.ppermute(a, "blk", [(i, i ^ 1) for i in range(agents)])

    def neighbours(half):
        got = along_z(half)
        both = (coef_own * half.astype(F32) + coef_got * got.astype(F32)).astype(BF)
        return along_x(both)

    contract = (((0,), (0,)), ((), ()))
    gate = lax.dot_general(inputs, gate_rel, contract, preferred_element_type=F32)
    up = lax.dot_general(inputs, up_rel, contract, preferred_element_type=F32)
    hidden = (jax.nn.silu(gate) * up).astype(BF)
    (hidden,) = permute_rows([hidden], token_order, groups)

    def residual(half, target):
        out = scale * jnp.dot(hidden, half, preferred_element_type=F32)
        partial = (out - target.astype(F32)).astype(BF)
        return gather_blocks(scatter_sum(partial))

    def gradient(resid):
        return scale * lax.dot_general(hidden, resid, contract, preferred_element_type=F32)

    halves = [f.astype(BF) for f in field]
    mixed = [weight_self * f + neighbours(h).astype(F32) for f, h in zip(field, halves)]
    bases, tails, resids = [], [], []
    for i in range(CHUNKS):
        first = gradient(residual(halves[i], teach[i]))
        moved = (mixed[i] - step * first).astype(BF)
        combined = mixed[i] - (2.0 * step) * first
        tails.append(neighbours(combined.astype(BF)))
        bases.append(weight_self * combined + step * first)
        resids.append(residual(moved, teach[i]))
    second = gradient(jnp.concatenate(resids, axis=1))
    base = jnp.concatenate(bases, axis=1)
    tail = jnp.concatenate(tails, axis=1)
    return (base + tail.astype(F32) - step * second)[None]


def solution(mesh):
    placed = (
        P(None, "tp"),
        P(None, "tp"),
        P(None, "tp"),
        P(None, "tp"),
        P("blk", "tp", None),
        P(),
        P(),
        P(),
    )
    return jax.shard_map(
        body, mesh=mesh, in_specs=placed, out_specs=P("blk", "tp", None), check_vma=False
    )
```

```python
import jax
import jax.numpy as jnp
from jax import lax
from jax.experimental import pallas as pl
from jax.experimental.pallas import tpu as pltpu
from jax.sharding import PartitionSpec as P


NX, NY, NC = 2, 4, 2
BF = jnp.bfloat16
F32 = jnp.float32
barrier = lax.optimization_barrier


def tp_shift(dx, dy, dc):
    pairs = []
    for x in range(NX):
        for y in range(NY):
            for c in range(NC):
                to = ((x + dx) % NX * NY + (y + dy) % NY) * NC + (c + dc) % NC
                pairs.append(((x * NY + y) * NC + c, to))
    return pairs


def send(array, dx, dy, dc):
    return lax.ppermute(array, "tp", tp_shift(dx, dy, dc))


def hidden_kernel(feature_ref, token_ref, plane_ref, other_ref, gate_ref, up_ref, h_ref, ht_ref, x_ref):
    i = pl.program_id(0)
    blocks = NX * NY
    rows = plane_ref.shape[0] // blocks
    lanes = plane_ref.shape[1] // (NY * NC)
    per = h_ref.shape[0] // lanes
    for j in range(2 * blocks):
        source = plane_ref if j < blocks else other_ref
        at = pl.multiple_of(feature_ref[j] * rows, 16)
        for s in range(per):
            token = pl.multiple_of(token_ref[i * per + s] * lanes, 128)
            x_ref[pl.ds(at, rows), s * lanes : (s + 1) * lanes] = source[
                (j % blocks) * rows : (j % blocks + 1) * rows, pl.ds(token, lanes)
            ]
    x = x_ref[...]
    gate = jnp.dot(gate_ref[...], x, preferred_element_type=F32)
    up = jnp.dot(up_ref[...], x, preferred_element_type=F32)
    hidden = gate / (1.0 + jnp.exp(-gate)) * up
    ht_ref[...] = hidden.astype(BF)
    h_ref[...] = hidden.T.astype(BF)


def make_hidden(feature_order, token_order, plane, other, gate_t, up_t):
    units, features = gate_t.shape
    tokens = plane.shape[1]
    tile = 256
    whole = lambda i, f, t: (0, 0)
    return pl.pallas_call(
        hidden_kernel,
        out_shape=(
            jax.ShapeDtypeStruct((tokens, units), BF),
            jax.ShapeDtypeStruct((units, tokens), BF),
        ),
        grid_spec=pltpu.PrefetchScalarGridSpec(
            num_scalar_prefetch=2,
            grid=(tokens // tile,),
            in_specs=[
                pl.BlockSpec(plane.shape, whole),
                pl.BlockSpec(other.shape, whole),
                pl.BlockSpec(gate_t.shape, whole),
                pl.BlockSpec(up_t.shape, whole),
            ],
            out_specs=[
                pl.BlockSpec((tile, units), lambda i, f, t: (i, 0)),
                pl.BlockSpec((units, tile), lambda i, f, t: (0, i)),
            ],
            scratch_shapes=[pltpu.VMEM((features, tile), BF)],
        ),
        cost_estimate=pl.CostEstimate(
            flops=4 * units * features * tokens,
            transcendentals=units * tokens,
            bytes_accessed=2 * (2 * units * features + features * tokens + 2 * units * tokens),
        ),
        name="make_hidden",
    )(feature_order, token_order, plane, other, gate_t, up_t)


def total(*terms):
    out = terms[0].astype(F32)
    for term in terms[1:]:
        out = out + term.astype(F32)
    return out


def sum_over_units(partial):
    half = partial.shape[0] // NC
    quarter = half // NY
    got = send(partial[half:], 0, 0, 1)
    rest = total(partial[quarter:half], got[quarter:]).astype(BF)
    parts = [send(rest[(d - 1) * quarter : d * quarter], 0, d, 0) for d in (1, 3, 2)]
    mine = total(partial[:quarter], got[:quarter], *parts)
    mine_half = mine.astype(BF)
    mine = total(mine, send(mine_half, 1, 0, 0)).astype(BF)
    back = [send(mine, 0, -d, 0) for d in (1, 3, 2)]
    plane = jnp.concatenate([mine, back[0], back[2], back[1]], axis=0)
    return jnp.concatenate([plane, send(plane, 0, 0, 1)], axis=0)


def body(
    input_pool, teacher_pool, gate_weight, up_weight, params, batch_ids, cycle_order, edge_weight
):
    step = 2.0
    groups = lax.axis_size("tp")
    agents = cycle_order.shape[0]
    place = lax.axis_index("blk")
    at = lax.axis_index("tp")
    core, y, xh = at % NC, (at // NC) % NY, at // (NC * NY)
    slots = jnp.arange(agents, dtype=jnp.int32)

    def edge(offset):
        return jnp.sum(jnp.where(slots == (place + offset) % agents, edge_weight, 0.0))

    weight_next, weight_prev = edge(0), edge(agents - 1)
    weight_self = 1.0 - weight_next - weight_prev
    odd = place % 2 == 1
    coef_own = jnp.where(odd, weight_prev, weight_next)
    coef_got = jnp.where(odd, edge(agents - 2), edge(1))
    agent = jnp.sum(jnp.where(slots == place, cycle_order, 0))
    batch = lax.dynamic_slice_in_dim(batch_ids, agent, 1, 0)[0]

    order = jnp.arange(groups, dtype=jnp.int32)
    dc, dy, dx = order // (NY * NX), (order // NX) % NY, order % NX
    feature_order = ((xh + dx) % NX * NY + (y + dy) % NY) * NC + (core + dc) % NC
    order = jnp.arange(NC * NY, dtype=jnp.int32)
    token_order = (core + order // NY) % NC * NY + (y + order % NY) % NY

    hidden_dev, features = gate_weight.shape[1], gate_weight.shape[0]
    cut = (hidden_dev // 2 + 15) // 16 * 16
    pieces = [slice(0, cut), slice(cut, hidden_dev)]
    zmove = [(i, (i + 2) % agents if i % 2 else (i - 2) % agents) for i in range(agents)]
    xmove = [(i, i ^ 1) for i in range(agents)]

    def along_z(half):
        out = []
        for s in pieces:
            out.append(lax.ppermute(half[s], "blk", zmove))
        return out

    def along_x(half, got, i):
        both = total(coef_own * half[pieces[i]].astype(F32), coef_got * got.astype(F32)).astype(BF)
        return lax.ppermute(both, "blk", xmove)

    rows = jnp.take(input_pool, batch, axis=0).T
    rows, field = barrier((rows, params[0]))
    field_half = field.astype(BF)
    partner = send(rows, 1, 0, 0)
    got = along_z(field_half)
    partner, batch = barrier((partner, batch))
    pair = jnp.concatenate([rows, partner], axis=0)
    parts = [send(pair, 0, -d, 0) for d in (1, 3, 2)]

    batch_rel = jnp.take(batch.reshape(NC * NY, -1), token_order, axis=0).reshape(-1)
    teacher = jnp.take(teacher_pool, batch_rel, axis=0)
    width = teacher.shape[1]
    place_in = (
        lax.broadcasted_iota(jnp.int32, (width, features), 0) + at * width
        == lax.broadcasted_iota(jnp.int32, (width, features), 1)
    ).astype(BF)
    teacher_wide = jnp.dot(teacher, place_in, preferred_element_type=F32).astype(BF)

    parts, teacher_wide = barrier((parts, teacher_wide))
    plane = jnp.concatenate([pair, parts[0], parts[2], parts[1]], axis=0)
    plane, got[0] = barrier((plane, got[0]))
    other = send(plane, 0, 0, 1)
    side = [along_x(field_half, got[0], 0)]
    hidden, hidden_t = make_hidden(
        feature_order, token_order, plane, other, gate_weight.T, up_weight.T
    )
    hidden, got[1] = barrier((hidden, got[1]))
    side.append(along_x(field_half, got[1], 1))
    scale = float(hidden_dev * groups) ** (-0.5)

    def partial_out(half):
        out = scale * jnp.dot(hidden, half, preferred_element_type=F32)
        return (out - teacher_wide.astype(F32)).astype(BF)

    def gradient(resid):
        return scale * jnp.dot(hidden_t, resid, preferred_element_type=F32)

    resid = sum_over_units(partial_out(field_half))
    mixed = weight_self * field + jnp.concatenate(side, axis=0).astype(F32)
    first = gradient(resid)
    combined = mixed - (2.0 * step) * first
    combined_half = combined.astype(BF)
    got = along_z(combined_half)
    moved = (mixed - step * first).astype(BF)
    base = weight_self * combined + step * first
    side = [along_x(combined_half, g, i) for i, g in enumerate(got)]
    second = gradient(sum_over_units(partial_out(moved)))
    return (base + jnp.concatenate(side, axis=0).astype(F32) - step * second)[None]


def solution(mesh):
    placed = (
        P(None, "tp"),
        P(None, "tp"),
        P(None, "tp"),
        P(None, "tp"),
        P("blk", "tp", None),
        P(),
        P(),
        P(),
    )

    return jax.shard_map(
        body, mesh=mesh, in_specs=placed, out_specs=P("blk", "tp", None), check_vma=False
    )
```

```python
import jax
import jax.numpy as jnp
from jax import lax
from jax.experimental import pallas as pl
from jax.experimental.pallas import tpu as pltpu
from jax.sharding import PartitionSpec as P


NX, NY, NC = 2, 4, 2
BF = jnp.bfloat16
F32 = jnp.float32
barrier = lax.optimization_barrier


def tp_shift(dx, dy, dc):
    pairs = []
    for x in range(NX):
        for y in range(NY):
            for c in range(NC):
                to = ((x + dx) % NX * NY + (y + dy) % NY) * NC + (c + dc) % NC
                pairs.append(((x * NY + y) * NC + c, to))
    return pairs


def send(array, dx, dy, dc):
    return lax.ppermute(array, "tp", tp_shift(dx, dy, dc))


def hidden_kernel(feature_ref, token_ref, plane_ref, other_ref, gate_ref, up_ref, h_ref, ht_ref, x_ref):
    i = pl.program_id(0)
    blocks = NX * NY
    rows = plane_ref.shape[0] // blocks
    lanes = plane_ref.shape[1] // (NY * NC)
    per = h_ref.shape[0] // lanes
    for j in range(2 * blocks):
        source = plane_ref if j < blocks else other_ref
        at = pl.multiple_of(feature_ref[j] * rows, 16)
        for s in range(per):
            token = pl.multiple_of(token_ref[i * per + s] * lanes, 128)
            x_ref[pl.ds(at, rows), s * lanes : (s + 1) * lanes] = source[
                (j % blocks) * rows : (j % blocks + 1) * rows, pl.ds(token, lanes)
            ]
    x = x_ref[...]
    gate = jnp.dot(gate_ref[...], x, preferred_element_type=F32)
    up = jnp.dot(up_ref[...], x, preferred_element_type=F32)
    hidden = gate / (1.0 + jnp.exp(-gate)) * up
    ht_ref[...] = hidden.astype(BF)
    h_ref[...] = hidden.T.astype(BF)


def make_hidden(feature_order, token_order, plane, other, gate_t, up_t):
    units, features = gate_t.shape
    tokens = plane.shape[1]
    tile = 256
    whole = lambda i, f, t: (0, 0)
    return pl.pallas_call(
        hidden_kernel,
        out_shape=(
            jax.ShapeDtypeStruct((tokens, units), BF),
            jax.ShapeDtypeStruct((units, tokens), BF),
        ),
        grid_spec=pltpu.PrefetchScalarGridSpec(
            num_scalar_prefetch=2,
            grid=(tokens // tile,),
            in_specs=[
                pl.BlockSpec(plane.shape, whole),
                pl.BlockSpec(other.shape, whole),
                pl.BlockSpec(gate_t.shape, whole),
                pl.BlockSpec(up_t.shape, whole),
            ],
            out_specs=[
                pl.BlockSpec((tile, units), lambda i, f, t: (i, 0)),
                pl.BlockSpec((units, tile), lambda i, f, t: (0, i)),
            ],
            scratch_shapes=[pltpu.VMEM((features, tile), BF)],
        ),
        cost_estimate=pl.CostEstimate(
            flops=4 * units * features * tokens,
            transcendentals=units * tokens,
            bytes_accessed=2 * (2 * units * features + features * tokens + 2 * units * tokens),
        ),
        name="make_hidden",
    )(feature_order, token_order, plane, other, gate_t, up_t)


def stack_kernel(*refs):
    count = len(refs) - 2
    out, sems = refs[count], refs[count + 1]
    rows = refs[0].shape[0]
    copies = [
        pltpu.make_async_copy(refs[i], out.at[pl.ds(i * rows, rows)], sems.at[i])
        for i in range(count)
    ]
    for copy in copies:
        copy.start()
    for copy in copies:
        copy.wait()


def stack(parts):
    rows, width = parts[0].shape
    return pl.pallas_call(
        stack_kernel,
        out_shape=jax.ShapeDtypeStruct((rows * len(parts), width), parts[0].dtype),
        in_specs=[pl.BlockSpec(memory_space=pl.ANY)] * len(parts),
        out_specs=pl.BlockSpec(memory_space=pl.ANY),
        scratch_shapes=[pltpu.SemaphoreType.DMA((len(parts),))],
        name="stack",
    )(*parts)


def total(*terms):
    out = terms[0].astype(F32)
    for term in terms[1:]:
        out = out + term.astype(F32)
    return out


def sum_over_units(partial):
    half = partial.shape[0] // NC
    quarter = half // NY
    got = send(partial[half:], 0, 0, 1)
    rest = total(partial[quarter:half], got[quarter:]).astype(BF)
    parts = [send(rest[(d - 1) * quarter : d * quarter], 0, d, 0) for d in (1, 3, 2)]
    mine = total(partial[:quarter], got[:quarter], *parts)
    mine_half = mine.astype(BF)
    mine = total(mine, send(mine_half, 1, 0, 0)).astype(BF)
    back = [send(mine, 0, -d, 0) for d in (1, 3, 2)]
    plane = jnp.concatenate([mine, back[0], back[2], back[1]], axis=0)
    return jnp.concatenate([plane, send(plane, 0, 0, 1)], axis=0)


def body(
    input_pool, teacher_pool, gate_weight, up_weight, params, batch_ids, cycle_order, edge_weight
):
    step = 2.0
    groups = lax.axis_size("tp")
    agents = cycle_order.shape[0]
    place = lax.axis_index("blk")
    at = lax.axis_index("tp")
    core, y, xh = at % NC, (at // NC) % NY, at // (NC * NY)
    slots = jnp.arange(agents, dtype=jnp.int32)

    def edge(offset):
        return jnp.sum(jnp.where(slots == (place + offset) % agents, edge_weight, 0.0))

    weight_next, weight_prev = edge(0), edge(agents - 1)
    weight_self = 1.0 - weight_next - weight_prev
    odd = place % 2 == 1
    weight_near = jnp.where(odd, weight_prev, weight_next)
    weight_far = jnp.where(odd, weight_next, weight_prev)
    agent = jnp.sum(jnp.where(slots == place, cycle_order, 0))
    batch = lax.dynamic_slice_in_dim(batch_ids, agent, 1, 0)[0]

    order = jnp.arange(groups, dtype=jnp.int32)
    dc, dy, dx = order // (NY * NX), (order // NX) % NY, order % NX
    feature_order = ((xh + dx) % NX * NY + (y + dy) % NY) * NC + (core + dc) % NC
    order = jnp.arange(NC * NY, dtype=jnp.int32)
    token_order = (core + order // NY) % NC * NY + (y + order % NY) % NY

    hidden_dev, features = gate_weight.shape[1], gate_weight.shape[0]
    ends = [0] + [(hidden_dev * n // 3 + 15) // 16 * 16 for n in (1, 2)] + [hidden_dev]
    pieces = [slice(*e) for e in zip(ends, ends[1:])]
    zmove = [(i, (i - 2) % agents if i % 2 else (i + 2) % agents) for i in range(agents)]
    xmove = [(i, i ^ 1) for i in range(agents)]

    def neighbours(half):
        near, far = [], []
        for i, s in enumerate(pieces):
            near.append(lax.ppermute(half[s], "blk", xmove))
            far.append(lax.ppermute(near[i], "blk", zmove))
        near, far = jnp.concatenate(near, axis=0), jnp.concatenate(far, axis=0)
        return weight_near * near.astype(F32) + weight_far * far.astype(F32)

    rows = jnp.take(input_pool, batch, axis=0).T
    rows, field, batch = barrier((rows, params[0], batch))
    field_half = field.astype(BF)
    parts = [
        rows if dx + dy == 0 else send(rows, -dx, -dy, 0)
        for dy in range(NY)
        for dx in range(NX)
    ]

    batch_rel = jnp.take(batch.reshape(NC * NY, -1), token_order, axis=0).reshape(-1)
    teacher = jnp.take(teacher_pool, batch_rel, axis=0)
    width = teacher.shape[1]
    place_in = (
        lax.broadcasted_iota(jnp.int32, (width, features), 0) + at * width
        == lax.broadcasted_iota(jnp.int32, (width, features), 1)
    ).astype(BF)
    teacher_wide = jnp.dot(teacher, place_in, preferred_element_type=F32).astype(BF)

    parts, teacher_wide = barrier((parts, teacher_wide))
    plane = stack(parts)
    other = send(plane, 0, 0, 1)
    hidden, hidden_t = make_hidden(
        feature_order, token_order, plane, other, gate_weight.T, up_weight.T
    )
    scale = float(hidden_dev * groups) ** (-0.5)

    def partial_out(half):
        out = scale * jnp.dot(hidden, half, preferred_element_type=F32)
        return (out - teacher_wide.astype(F32)).astype(BF)

    def gradient(resid):
        return scale * jnp.dot(hidden_t, resid, preferred_element_type=F32)

    resid = sum_over_units(partial_out(field_half))
    mixed = weight_self * field + neighbours(field_half)
    first = gradient(resid)
    combined = mixed - (2.0 * step) * first
    around = neighbours(combined.astype(BF))
    moved = (mixed - step * first).astype(BF)
    base = weight_self * combined + step * first
    second = gradient(sum_over_units(partial_out(moved)))
    return (base + around - step * second)[None]


def solution(mesh):
    placed = (
        P(None, "tp"),
        P(None, "tp"),
        P(None, "tp"),
        P(None, "tp"),
        P("blk", "tp", None),
        P(),
        P(),
        P(),
    )

    return jax.shard_map(
        body, mesh=mesh, in_specs=placed, out_specs=P("blk", "tp", None), check_vma=False
    )
```

```python
import jax
import jax.numpy as jnp
from jax import lax
from jax.experimental import pallas as pl
from jax.experimental.pallas import tpu as pltpu
from jax.sharding import PartitionSpec as P


NX, NY, NC = 2, 4, 2
BF = jnp.bfloat16
F32 = jnp.float32
barrier = lax.optimization_barrier


def tp_shift(dx, dy, dc):
    pairs = []
    for x in range(NX):
        for y in range(NY):
            for c in range(NC):
                to = ((x + dx) % NX * NY + (y + dy) % NY) * NC + (c + dc) % NC
                pairs.append(((x * NY + y) * NC + c, to))
    return pairs


def send(array, dx, dy, dc):
    return lax.ppermute(array, "tp", tp_shift(dx, dy, dc))


def hidden_kernel(feature_ref, token_ref, plane_ref, other_ref, gate_ref, up_ref, h_ref, ht_ref, x_ref):
    i = pl.program_id(0)
    blocks = NX * NY
    rows = plane_ref.shape[0] // blocks
    lanes = plane_ref.shape[1] // (NY * NC)
    per = h_ref.shape[0] // lanes
    for j in range(2 * blocks):
        source = plane_ref if j < blocks else other_ref
        at = pl.multiple_of(feature_ref[j] * rows, 16)
        for s in range(per):
            token = pl.multiple_of(token_ref[i * per + s] * lanes, 128)
            x_ref[pl.ds(at, rows), s * lanes : (s + 1) * lanes] = source[
                (j % blocks) * rows : (j % blocks + 1) * rows, pl.ds(token, lanes)
            ]
    x = x_ref[...]
    gate = jnp.dot(gate_ref[...], x, preferred_element_type=F32)
    up = jnp.dot(up_ref[...], x, preferred_element_type=F32)
    hidden = gate / (1.0 + jnp.exp(-gate)) * up
    ht_ref[...] = hidden.astype(BF)
    h_ref[...] = hidden.T.astype(BF)


def make_hidden(feature_order, token_order, plane, other, gate_t, up_t):
    units, features = gate_t.shape
    tokens = plane.shape[1]
    tile = 256
    whole = lambda i, f, t: (0, 0)
    return pl.pallas_call(
        hidden_kernel,
        out_shape=(
            jax.ShapeDtypeStruct((tokens, units), BF),
            jax.ShapeDtypeStruct((units, tokens), BF),
        ),
        grid_spec=pltpu.PrefetchScalarGridSpec(
            num_scalar_prefetch=2,
            grid=(tokens // tile,),
            in_specs=[
                pl.BlockSpec(plane.shape, whole),
                pl.BlockSpec(other.shape, whole),
                pl.BlockSpec(gate_t.shape, whole),
                pl.BlockSpec(up_t.shape, whole),
            ],
            out_specs=[
                pl.BlockSpec((tile, units), lambda i, f, t: (i, 0)),
                pl.BlockSpec((units, tile), lambda i, f, t: (0, i)),
            ],
            scratch_shapes=[pltpu.VMEM((features, tile), BF)],
        ),
        cost_estimate=pl.CostEstimate(
            flops=4 * units * features * tokens,
            transcendentals=units * tokens,
            bytes_accessed=2 * (2 * units * features + features * tokens + 2 * units * tokens),
        ),
        name="make_hidden",
    )(feature_order, token_order, plane, other, gate_t, up_t)


def stack_kernel(*refs):
    out = refs[-1]
    rows = refs[0].shape[0]
    for i, part in enumerate(refs[:-1]):
        out[i * rows : (i + 1) * rows] = part[...]


def stack(parts):
    rows, width = parts[0].shape
    tile = width // 2
    size = 2 * rows * len(parts) * width * parts[0].dtype.itemsize
    return pl.pallas_call(
        stack_kernel,
        out_shape=jax.ShapeDtypeStruct((rows * len(parts), width), parts[0].dtype),
        grid=(width // tile,),
        in_specs=[pl.BlockSpec((rows, tile), lambda i: (0, i))] * len(parts),
        out_specs=pl.BlockSpec((rows * len(parts), tile), lambda i: (0, i)),
        cost_estimate=pl.CostEstimate(flops=0, transcendentals=0, bytes_accessed=size),
        name="stack",
    )(*parts)


def total(*terms):
    out = terms[0].astype(F32)
    for term in terms[1:]:
        out = out + term.astype(F32)
    return out


def sum_over_units(partial):
    half = partial.shape[0] // NC
    quarter = half // NY
    got = send(partial[half:], 0, 0, 1)
    rest = total(partial[quarter:half], got[quarter:]).astype(BF)
    parts = [send(rest[(d - 1) * quarter : d * quarter], 0, d, 0) for d in (1, 3, 2)]
    mine = total(partial[:quarter], got[:quarter], *parts)
    mine_half = mine.astype(BF)
    mine = total(mine, send(mine_half, 1, 0, 0)).astype(BF)
    back = [send(mine, 0, -d, 0) for d in (1, 3, 2)]
    plane = jnp.concatenate([mine, back[0], back[2], back[1]], axis=0)
    return jnp.concatenate([plane, send(plane, 0, 0, 1)], axis=0)


def body(
    input_pool, teacher_pool, gate_weight, up_weight, params, batch_ids, cycle_order, edge_weight
):
    step = 2.0
    groups = lax.axis_size("tp")
    agents = cycle_order.shape[0]
    place = lax.axis_index("blk")
    at = lax.axis_index("tp")
    core, y, xh = at % NC, (at // NC) % NY, at // (NC * NY)
    slots = jnp.arange(agents, dtype=jnp.int32)

    def edge(offset):
        return jnp.sum(jnp.where(slots == (place + offset) % agents, edge_weight, 0.0))

    weight_next, weight_prev = edge(0), edge(agents - 1)
    weight_self = 1.0 - weight_next - weight_prev
    odd = place % 2 == 1
    weight_near = jnp.where(odd, weight_prev, weight_next)
    weight_far = jnp.where(odd, weight_next, weight_prev)
    agent = jnp.sum(jnp.where(slots == place, cycle_order, 0))
    batch = lax.dynamic_slice_in_dim(batch_ids, agent, 1, 0)[0]

    order = jnp.arange(groups, dtype=jnp.int32)
    dc, dy, dx = order // (NY * NX), (order // NX) % NY, order % NX
    feature_order = ((xh + dx) % NX * NY + (y + dy) % NY) * NC + (core + dc) % NC
    order = jnp.arange(NC * NY, dtype=jnp.int32)
    token_order = (core + order // NY) % NC * NY + (y + order % NY) % NY

    hidden_dev, features = gate_weight.shape[1], gate_weight.shape[0]
    ends = [0] + [(hidden_dev * n // 3 + 15) // 16 * 16 for n in (1, 2)] + [hidden_dev]
    pieces = [slice(*e) for e in zip(ends, ends[1:])]
    zmove = [(i, (i - 2) % agents if i % 2 else (i + 2) % agents) for i in range(agents)]
    xmove = [(i, i ^ 1) for i in range(agents)]

    def neighbours(half):
        near, far = [], []
        for i, s in enumerate(pieces):
            near.append(lax.ppermute(half[s], "blk", xmove))
            far.append(lax.ppermute(near[i], "blk", zmove))
        near, far = jnp.concatenate(near, axis=0), jnp.concatenate(far, axis=0)
        return weight_near * near.astype(F32) + weight_far * far.astype(F32)

    rows = jnp.take(input_pool, batch, axis=0).T
    rows, field, batch = barrier((rows, params[0], batch))
    field_half = field.astype(BF)
    parts = [
        rows if dx + dy == 0 else send(rows, -dx, -dy, 0)
        for dy in range(NY)
        for dx in range(NX)
    ]

    batch_rel = jnp.take(batch.reshape(NC * NY, -1), token_order, axis=0).reshape(-1)
    teacher = jnp.take(teacher_pool, batch_rel, axis=0)
    width = teacher.shape[1]
    place_in = (
        lax.broadcasted_iota(jnp.int32, (width, features), 0) + at * width
        == lax.broadcasted_iota(jnp.int32, (width, features), 1)
    ).astype(BF)
    teacher_wide = jnp.dot(teacher, place_in, preferred_element_type=F32).astype(BF)

    parts, teacher_wide = barrier((parts, teacher_wide))
    plane = stack(parts)
    other = send(plane, 0, 0, 1)
    hidden, hidden_t = make_hidden(
        feature_order, token_order, plane, other, gate_weight.T, up_weight.T
    )
    scale = float(hidden_dev * groups) ** (-0.5)

    def partial_out(half):
        out = scale * jnp.dot(hidden, half, preferred_element_type=F32)
        return (out - teacher_wide.astype(F32)).astype(BF)

    def gradient(resid):
        return scale * jnp.dot(hidden_t, resid, preferred_element_type=F32)

    resid = sum_over_units(partial_out(field_half))
    mixed = weight_self * field + neighbours(field_half)
    first = gradient(resid)
    combined = mixed - (2.0 * step) * first
    around = neighbours(combined.astype(BF))
    moved = (mixed - step * first).astype(BF)
    base = weight_self * combined + step * first
    second = gradient(sum_over_units(partial_out(moved)))
    return (base + around - step * second)[None]


def solution(mesh):
    placed = (
        P(None, "tp"),
        P(None, "tp"),
        P(None, "tp"),
        P(None, "tp"),
        P("blk", "tp", None),
        P(),
        P(),
        P(),
    )

    return jax.shard_map(
        body, mesh=mesh, in_specs=placed, out_specs=P("blk", "tp", None), check_vma=False
    )
```
